256 devices in a mesh: gx: 32 (over x, z), gy: 8 (over y, core).
Axes of the slice: x: 4, y: 4, z: 8, core: 2. Of those that a mesh axis runs over, the one named last changes fastest.
Arguments:
- self_blk: float32 [512, 128, 128], P(('gx', 'gy')), may hold values from -6 to 6
- near: bfloat16 [512, 14, 512, 128], P(('gx', 'gy')), may hold values from -0.59765625 to 0.59765625
- back: bfloat16 [512, 14, 128, 512], P(('gx', 'gy')), may hold values from -0.59765625 to 0.59765625
- interp: bfloat16 [512, 128, 512], P(('gx', 'gy')), may hold values from -0.59765625 to 0.59765625
- redinv: bfloat16 [512, 512, 512], P(('gx', 'gy')), as said below
- ranks: int32 [512], P(('gx', 'gy')), may hold values from 64 to 128, as said below
- pivots: int32 [512, 128], P(('gx', 'gy')), may hold values from 0 to 511, as said below
- neighbors: int32 [512, 14], P(('gx', 'gy')), may hold values from 0 to 511, as said below
- parent: int32 [512], P(('gx', 'gy')), may hold values from 0 to 511, as said below
Outputs:
- parent_blocks: float32 [512, 128, 128], P(('gx', 'gy'))
The draws below stay inside these ranges and needn't reach their ends.
Inputs may be any that keep to these rules, and one draw needn't show every extreme that they name: redinv is used only on a box's redundant points. `ranks`: every draw has a box of rank 128 and a box of rank 64. `pivots`: the 128 entries of a box are distinct; the first ranks[b] of them are its skeleton points, the others are redundant points. `neighbors`: box b lies on the device of linear index b // 2, gx major. A box's neighbours are distinct, never the box itself, and lie on devices of the same gy index. The entries of the 2 boxes of one device name boxes of any one device at most 4 times; in every draw and every gy index one device is named exactly 4 times by each other device of that gy index. `parent`: A permutation of the boxes that maps the 16 boxes of each gx index onto the same 16 rows.
All inputs are finite; a program needn't handle non-finite values.
Results may differ from the reference program's by a relative error of at most 0.0049.
Values may be sent and summed in bfloat16 or wider, within the bound.
A program may use at most 64 MiB of HBM per device.

```python
import math
import jax
import jax.numpy as jnp
from jax import lax

P_SIZE = 512
K = 128
NB = 14
BOX_DEV = 2
KMIN = 64
PEERS = 32
LANES = 8
ROW_BOXES = 16
BOXES = 512


def draw_redinv(key, part):
    sub = jax.random.fold_in(key, 15)
    noise = 0.5 * jax.random.normal(sub, (BOXES, P_SIZE, P_SIZE), jnp.float32)
    full = jnp.eye(P_SIZE, dtype=jnp.float32)[None] + noise / math.sqrt(P_SIZE)
    return full.astype(jnp.bfloat16)


def draw_ranks(key, part):
    base = jax.random.fold_in(key, 11)
    values = jax.random.randint(jax.random.fold_in(base, 1), (BOXES,), KMIN, K + 1)
    highest = jax.random.randint(jax.random.fold_in(base, 2), (), 0, BOXES)
    lowest = (highest + 1 + jax.random.randint(jax.random.fold_in(base, 3), (), 0, BOXES - 1)) % BOXES
    values = values.at[highest].set(K)
    values = values.at[lowest].set(KMIN)
    return values.astype(jnp.int32)


def draw_pivots(key, part):
    keys = jax.random.split(jax.random.fold_in(key, 12), BOXES)

    def one_box(sub):
        return jax.random.permutation(sub, P_SIZE)[:K]
    return jax.vmap(one_box)(keys).astype(jnp.int32)


def draw_neighbors(key, part):
    base = jax.random.fold_in(key, 13)
    hottest = jax.random.randint(jax.random.fold_in(base, 1), (LANES,), 0, PEERS)
    keys = jax.random.split(jax.random.fold_in(base, 2), BOXES)
    column = PEERS * BOX_DEV
    candidates = jnp.arange(column, dtype=jnp.int32)

    def one_box(sub, box):
        device = box // BOX_DEV
        slot = box % BOX_DEV
        gx_row = device // LANES
        lane = device % LANES
        first_key, second_key = jax.random.split(sub)
        scores = jax.random.permutation(first_key, column).astype(jnp.int32)
        on_hot = candidates // BOX_DEV == hottest[lane]
        scores = jnp.where(on_hot, -1, scores)
        scores = jnp.where(candidates == gx_row * BOX_DEV + slot, column + 1, scores)
        ordered = jnp.argsort(scores, stable=True)[:NB]
        mixing = jax.random.permutation(second_key, NB)
        chosen = ordered[mixing].astype(jnp.int32)
        target_device = chosen // BOX_DEV * LANES + lane
        return (target_device * BOX_DEV + chosen % BOX_DEV).astype(jnp.int32)
    return jax.vmap(one_box)(keys, jnp.arange(BOXES, dtype=jnp.int32))


def draw_parent(key, part):
    keys = jax.random.split(jax.random.fold_in(key, 14), PEERS)

    def one_row(sub):
        return jax.random.permutation(sub, ROW_BOXES).astype(jnp.int32)
    perms = jax.vmap(one_row)(keys)
    offsets = (jnp.arange(PEERS, dtype=jnp.int32) * ROW_BOXES)[:, None]
    return (perms + offsets).reshape(BOXES).astype(jnp.int32)


def level_of(key, extent, cuts, low, largest):
    gain = 1.0
    for position, parts in cuts:
        steps = jax.random.uniform(jax.random.fold_in(jax.random.fold_in(key, 6), position), (parts,), jnp.float32, low / len(cuts), largest / len(cuts))
        gain = gain * jnp.repeat(jnp.exp(steps), extent[position] // parts).reshape((-1,) + (1,) * (len(extent) - 1 - position))
    return gain


def normal_values(key, shape, scale, reach, pieces=(), kind=jnp.bfloat16):
    drawn = scale * jax.random.normal(key, shape, jnp.float32)
    if pieces:
        drawn = drawn * level_of(key, shape, pieces, -0.22, 0.18)
    return jnp.clip(drawn, -reach, reach).astype(kind)


def setup_inputs(seed: int = 0) -> dict:
    seeds = jax.random.split(jax.random.key(seed), 10)
    return {
        "self_blk": normal_values(seeds[0], (BOXES, K, K), 1.0, 6.0, ((0, 256),), jnp.float32),
        "near": normal_values(seeds[1], (BOXES, NB, P_SIZE, K), 0.1, 0.59765625, ((0, 256),)),
        "back": normal_values(seeds[2], (BOXES, NB, K, P_SIZE), 0.1, 0.59765625, ((0, 256),)),
        "interp": normal_values(seeds[3], (BOXES, K, P_SIZE), 0.1, 0.59765625, ((0, 256),)),
        "redinv": draw_redinv(jax.random.fold_in(seeds[9], 71), 0),
        "ranks": draw_ranks(jax.random.fold_in(seeds[9], 71), 0),
        "pivots": draw_pivots(jax.random.fold_in(seeds[9], 71), 0),
        "neighbors": draw_neighbors(jax.random.fold_in(seeds[9], 71), 0),
        "parent": draw_parent(jax.random.fold_in(seeds[9], 71), 0),
    }


def box_updates(near_b, back_b, interp_b, redinv_b, rank_b, pivot_b):
    points = jnp.arange(P_SIZE, dtype=jnp.int32)
    living = jnp.arange(K, dtype=jnp.int32) < rank_b
    select = jnp.where((pivot_b[:, None] == points[None, :]) & living[:, None], 1.0, 0.0).astype(jnp.float32)
    redundant = 1.0 - jnp.sum(select, axis=0)
    alive_rows = jnp.where(living, 1.0, 0.0).astype(jnp.float32)
    coefficients = interp_b.astype(jnp.float32) * alive_rows[:, None] * redundant[None, :]
    placed = jnp.dot(coefficients.T, select, precision=lax.Precision.HIGHEST)
    compress = (redundant[:, None] * (jnp.eye(P_SIZE, dtype=jnp.float32) - placed)).astype(jnp.bfloat16)
    halfway = jnp.dot(redinv_b, compress, preferred_element_type=jnp.float32).astype(jnp.bfloat16)
    eliminator = jnp.dot(compress.T, halfway, preferred_element_type=jnp.float32).astype(jnp.bfloat16)
    lifted = jnp.einsum('nkp,pq->nkq', back_b.astype(jnp.float32), eliminator.astype(jnp.float32),
                        precision=lax.Precision.HIGHEST).astype(jnp.bfloat16)
    lifted = lax.optimization_barrier(lifted)
    return -jnp.einsum('nkq,nql->nkl', lifted.astype(jnp.float32), near_b.astype(jnp.float32),
                       precision=lax.Precision.HIGHEST)


def reference(self_blk, near, back, interp, redinv, ranks, pivots, neighbors, parent):
    device_total = BOXES // BOX_DEV
    entry_count = BOX_DEV * NB

    def device_step(summed, device_index):
        first_box = (device_index * BOX_DEV).astype(jnp.int32)

        def window(array):
            return lax.dynamic_slice_in_dim(array, first_box, BOX_DEV, 0)

        updates = jax.vmap(box_updates)(window(near), window(back), window(interp), window(redinv),
                                        window(ranks), window(pivots))
        flattened = updates.reshape(entry_count, K * K)
        targets = window(neighbors).reshape(entry_count)
        same_target = jnp.where(targets[:, None] == targets[None, :], 1.0, 0.0).astype(jnp.float32)
        grouped = jnp.dot(same_target, flattened, precision=lax.Precision.HIGHEST).astype(jnp.bfloat16)
        grouped = lax.optimization_barrier(grouped)
        earlier = jnp.sum(jnp.tril(same_target, -1), axis=1)
        leading = jnp.where(earlier == 0.0, 1.0, 0.0).astype(jnp.float32)
        summed = summed.at[targets].add(grouped.astype(jnp.float32) * leading[:, None])
        return summed, None

    summed, unused = lax.scan(device_step, jnp.zeros((BOXES, K * K), jnp.float32),
                              jnp.arange(device_total, dtype=jnp.int32))
    living = jnp.arange(K, dtype=jnp.int32)[None, :] < ranks[:, None]
    masking = living[:, :, None] & living[:, None, :]
    schur = jnp.where(masking, self_blk + summed.reshape(BOXES, K, K), 0.0)
    return jnp.zeros_like(schur).at[parent].set(schur)
```

```python
import jax
import jax.numpy as jnp
from jax import lax
from jax.experimental import pallas as pl
from jax.experimental.pallas import tpu as pltpu
from jax.sharding import PartitionSpec as P

BF = jnp.bfloat16
F32 = jnp.float32
MESH = pl.DeviceIdType.MESH
NT = (((1,), (1,)), ((), ()))

XS, ZS, YS = 4, 8, 4
BOXES_HERE, NBR, K, PTS = 2, 14, 128, 512
ENTRIES = BOXES_HERE * NBR
HALF = K // 2


class Mail:
    def __init__(self, send_sem, recv_sem):
        self.send_sem, self.recv_sem, self.made = send_sem, recv_sem, []

    def post(self, src, dst, device):
        m = len(self.made)
        copy = pltpu.make_async_remote_copy(
            src_ref=src, dst_ref=dst, send_sem=self.send_sem.at[m],
            recv_sem=self.recv_sem.at[m], device_id=device, device_id_type=MESH)
        copy.start()
        self.made.append(copy)
        return copy


MESSAGES = 96


def make_eliminator(rank, pivot_row, interp, redinv):
    point = lax.broadcasted_iota(jnp.int32, (PTS, K), 0)
    lane = lax.broadcasted_iota(jnp.int32, (PTS, K), 1)
    select_t = jnp.where((point == pivot_row) & (lane < rank), 1.0, 0.0).astype(F32)
    skel_col = jnp.sum(select_t, axis=1, keepdims=True)
    select_t = select_t.astype(BF)
    skel_row = lax.dot_general(jnp.ones((8, K), BF), select_t, NT, preferred_element_type=F32)[0:1]
    living = lax.broadcasted_iota(jnp.int32, (K, PTS), 0) < rank
    coeff = jnp.where(living & (skel_row < 0.5), interp.astype(F32), 0.0).astype(BF)
    through = -lax.dot_general(redinv, coeff, NT, preferred_element_type=F32)
    spread = lax.dot_general(through.astype(BF), select_t, NT, preferred_element_type=F32)
    halfway = jnp.where(skel_row < 0.5, redinv.astype(F32), spread).astype(BF)
    folded = -jnp.dot(coeff, halfway, preferred_element_type=F32)
    placed = jnp.dot(select_t, folded.astype(BF), preferred_element_type=F32)
    return jnp.where(skel_col < 0.5, halfway.astype(F32), placed).astype(BF)


def kernel(self_h, near_h, back_h, interp_h, redinv_h, ranks_s, pivots_v, nbr_s, par_s,
           out_ref,
           self_v, near_v, back_v, interp_v, redinv_v, elim_v, upd_v, tab_v, tab_s,
           own_par, all_par, par_tab,
           out_a, out_b, ra2, ra1, acc_a, sa, rza, rzb, acc_b, sb, rxb, gath,
           load_sem, tab_sem, send_sem, recv_sem):
    gx, gy = lax.axis_index("gx"), lax.axis_index("gy")
    x, z = gx // ZS, gx % ZS
    y, c = gy // 2, gy % 2

    def row(dx, dz):
        return ((x + dx) % XS) * ZS + (z + dz) % ZS

    def lane(dy, dc):
        return ((y + dy) % YS) * 2 + (c + dc) % 2

    xp, xm = (row(1, 0), gy), (row(XS - 1, 0), gy)
    zp, zm = (row(0, 1), gy), (row(0, ZS - 1), gy)
    yp, ym = (gx, lane(1, 0)), (gx, lane(YS - 1, 0))
    twin = (gx, lane(0, 1))
    lanes = [(gx, lane(dy, dc)) for dy in range(YS) for dc in range(2) if dy or dc]

    barrier = pltpu.get_barrier_semaphore()
    partners = [xp, xm, zp, zm] + lanes
    for device in partners:
        pl.semaphore_signal(barrier, inc=1, device_id=device, device_id_type=MESH)

    loads = []

    def load(src, dst):
        copy = pltpu.make_async_copy(src, dst, load_sem.at[len(loads)])
        copy.start()
        loads.append(copy)
        return copy

    in_i, in_r, in_b, in_n = [], [], [], []
    for b in range(BOXES_HERE):
        in_i.append(load(interp_h.at[b], interp_v.at[b]))
        in_r.append(load(redinv_h.at[b], redinv_v.at[b]))
        in_b.append(load(back_h.at[b], back_v.at[b]))
        in_n.append(load(near_h.at[b], near_v.at[b]))
    in_s = load(self_h, self_v)

    slots = lax.broadcasted_iota(jnp.int32, (1, K), 1)
    for b in range(BOXES_HERE):
        table = jnp.full((1, K), ENTRIES, jnp.int32)
        for n in range(NBR):
            target = nbr_s[b, n]
            slot = (target // (BOXES_HERE * YS * 2)) * BOXES_HERE + target % BOXES_HERE
            table = jnp.where(slots == slot, b * NBR + n, table)
        tab_v[b:b + 1, :] = table
    for b in range(BOXES_HERE):
        own_par[b:b + 1, :] = jnp.full((1, K), par_s[b], jnp.int32)
    tab_copy = pltpu.make_async_copy(tab_v, tab_s, tab_sem.at[0])
    tab_copy.start()
    upd_v[ENTRIES] = jnp.zeros((K, K), F32)

    for b in range(BOXES_HERE):
        in_i[b].wait()
        in_r[b].wait()
        elim_v[b] = make_eliminator(ranks_s[b], pivots_v[b:b + 1, :], interp_v[b], redinv_v[b])
        in_b[b].wait()
        in_n[b].wait()

        def pair(i, carry, b=b):
            rows = back_v[b, pl.ds(2 * i, 2)].reshape(2 * K, PTS)
            lifted = jnp.dot(rows, elim_v[b], preferred_element_type=F32).astype(BF)
            for h in range(2):
                upd_v[b * NBR + 2 * i + h] = jnp.dot(
                    lifted[h * K:(h + 1) * K], near_v[b, 2 * i + h], preferred_element_type=F32)
            return carry

        lax.fori_loop(0, NBR // 2, pair, 0)

    tab_copy.wait()

    def assemble(r, carry):
        for slot in range(BOXES_HERE):
            s = BOXES_HERE * r + slot
            value = (-(upd_v[tab_s[0, s]] + upd_v[tab_s[1, s]])).astype(BF)
            if slot == 0:
                out_a[r // ZS, r % ZS] = value
            else:
                out_b[r % ZS, r // ZS] = value
        return carry

    lax.fori_loop(0, XS * ZS, assemble, 0)

    pl.semaphore_wait(barrier, len(partners))
    mail = Mail(send_sem, recv_sem)

    x1, x2, x3 = (x + 1) % XS, (x + 2) % XS, (x + 3) % XS
    lo, hi = pl.ds(0, ZS // 2), pl.ds(ZS // 2, ZS // 2)
    a2p = mail.post(out_a.at[x2, lo], ra2.at[0], xp)
    a2m = mail.post(out_a.at[x2, hi], ra2.at[1], xm)

    ha, hb = pl.ds(0, XS // 2), pl.ds(XS // 2, XS // 2)
    halves = (ha, hb)

    def post_b(d, h, k):
        target = (z + k) % ZS if d == 0 else (z + ZS - k) % ZS
        return mail.post(out_b.at[target, halves[h]], rzb.at[d, h, k - 1], zp if d == 0 else zm)

    def fold_b(d, h, k):
        target = (z + k) % ZS if d == 0 else (z + ZS - k) % ZS
        out_b[target, halves[h]] = out_b[target, halves[h]] + rzb[d, h, k]

    far = {}
    far[0, 0, 4] = post_b(0, 0, 4)
    far[1, 1, 4] = post_b(1, 1, 4)
    far[0, 1, 3] = post_b(0, 1, 3)
    far[1, 0, 3] = post_b(1, 0, 3)
    a1p = [mail.post(out_a.at[x1, hi], ra1.at[0, hi], xp)]
    a1m = [mail.post(out_a.at[x3, lo], ra1.at[1, lo], xm)]

    par_home = all_par.at[gy]
    own_copy = pltpu.make_async_copy(own_par, par_home, tab_sem.at[1])
    own_copy.start()
    par_mail = [mail.post(own_par, all_par.at[gy], device) for device in lanes]

    def hop_b(k):
        for d in range(2):
            h = d
            far[d, h, k + 1].wait_recv()
            fold_b(d, h, k)
            far[d, h, k] = post_b(d, h, k)
        if k > 1:
            for d in range(2):
                h = 1 - d
                far[d, h, k].wait_recv()
                fold_b(d, h, k - 1)
                far[d, h, k - 1] = post_b(d, h, k - 1)

    hop_b(3)

    a2p.wait_recv()
    out_a[x1, lo] = out_a[x1, lo] + ra2[0]
    a1p.append(mail.post(out_a.at[x1, lo], ra1.at[0, lo], xp))
    a2m.wait_recv()
    out_a[x3, hi] = out_a[x3, hi] + ra2[1]
    a1m.append(mail.post(out_a.at[x3, hi], ra1.at[1, hi], xm))

    hop_b(2)
    hop_b(1)

    for copy in a1p + a1m:
        copy.wait_recv()
    acc_a[...] = out_a[x].astype(F32) + ra1[0].astype(F32) + ra1[1].astype(F32)

    top, bottom = pl.ds(0, HALF), pl.ds(HALF, HALF)
    part = (top, bottom)

    def target_z(d, k):
        return (z + k) % ZS if d == 0 else (z + ZS - k) % ZS

    near_a = {}
    for d in range(2):
        sa[d, 3, part[d]] = acc_a[target_z(d, 4), part[d]].astype(BF)
        near_a[d, 4] = mail.post(sa.at[d, 3, part[d]], rza.at[d, 3, part[d]], zp if d == 0 else zm)

    def hop_a(k):
        for d in range(2):
            near_a[d, k + 1].wait_recv()
            t = target_z(d, k)
            if k == 3:
                sa[d, 2, part[d]] = (acc_a[t, part[d]] + rza[d, 3, part[d]].astype(F32)).astype(BF)
                sa[d, 2, part[1 - d]] = acc_a[t, part[1 - d]].astype(BF)
            else:
                sa[d, k - 1] = (acc_a[t] + rza[d, k].astype(F32)).astype(BF)
            near_a[d, k] = mail.post(sa.at[d, k - 1], rza.at[d, k - 1], zp if d == 0 else zm)

    for d in range(2):
        for h in range(2):
            far[d, h, 1].wait_recv()
    for h in range(2):
        acc_b[halves[h]] = (out_b[z, halves[h]].astype(F32) + rzb[0, h, 0].astype(F32)
                            + rzb[1, h, 0].astype(F32))

    def target_x(d, k):
        return (x + k) % XS if d == 0 else (x + XS - k) % XS

    near_b = {}
    for d in range(2):
        sb[d, 1, part[d]] = acc_b[target_x(d, 2), part[d]].astype(BF)
        near_b[d, 2] = mail.post(sb.at[d, 1, part[d]], rxb.at[d, 1, part[d]], xp if d == 0 else xm)

    hop_a(3)
    for d in range(2):
        near_b[d, 2].wait_recv()
        t = target_x(d, 1)
        sb[d, 0, part[d]] = (acc_b[t, part[d]] + rxb[d, 1, part[d]].astype(F32)).astype(BF)
        sb[d, 0, part[1 - d]] = acc_b[t, part[1 - d]].astype(BF)
        near_b[d, 1] = mail.post(sb.at[d, 0], rxb.at[d, 0], xp if d == 0 else xm)
    hop_a(2)

    in_s.wait()
    j = lax.broadcasted_iota(jnp.int32, (K, K), 0)
    l = lax.broadcasted_iota(jnp.int32, (K, K), 1)

    def finish(slot, total):
        rank = ranks_s[slot]
        merged = jnp.where((j < rank) & (l < rank), self_v[slot] + total, 0.0)
        gath[gy, slot] = merged.astype(BF)

    here = [gy, lane(YS - 1, 0), lane(1, 0), lane(2, 0)]

    def share(slot):
        return [mail.post(gath.at[gy, slot], gath.at[gy, slot], device) for device in (yp, ym, twin)]

    def forward(slot, sent):
        got = [sent[2]]
        sent[0].wait_recv()
        far_top = mail.post(gath.at[here[1], slot, top], gath.at[here[1], slot, top], yp)
        got.append(mail.post(gath.at[here[1], slot], gath.at[here[1], slot], twin))
        sent[1].wait_recv()
        far_bottom = mail.post(gath.at[here[2], slot, bottom], gath.at[here[2], slot, bottom], ym)
        got.append(mail.post(gath.at[here[2], slot], gath.at[here[2], slot], twin))
        return got, far_top, far_bottom

    def finish_forward(slot, state):
        got, far_top, far_bottom = state
        far_top.wait_recv()
        got.append(mail.post(gath.at[here[3], slot, top], gath.at[here[3], slot, top], twin))
        far_bottom.wait_recv()
        got.append(mail.post(gath.at[here[3], slot, bottom], gath.at[here[3], slot, bottom], twin))
        return got

    for d in range(2):
        near_b[d, 1].wait_recv()
    finish(1, acc_b[x] + rxb[0, 0].astype(F32) + rxb[1, 0].astype(F32))
    sent_b = share(1)
    hop_a(1)
    state_b = forward(1, sent_b)
    for d in range(2):
        near_a[d, 1].wait_recv()
    finish(0, acc_a[z] + rza[0, 0].astype(F32) + rza[1, 0].astype(F32))
    sent_a = share(0)
    got = finish_forward(1, state_b)
    state_a = forward(0, sent_a)

    own_copy.wait()
    for copy in par_mail:
        copy.wait_recv()
    par_copy = pltpu.make_async_copy(all_par, par_tab, tab_sem.at[2])
    par_copy.start()

    got += finish_forward(0, state_a)
    par_copy.wait()
    for copy in got:
        copy.wait_recv()
    first_row = gx * (YS * 2 * BOXES_HERE) + gy * BOXES_HERE
    for q in range(BOXES_HERE):
        found_lane, found_slot = jnp.int32(0), jnp.int32(0)
        for k in range(YS * 2):
            for s in range(BOXES_HERE):
                hit = par_tab[k, s, 0] == first_row + q
                found_lane = jnp.where(hit, k, found_lane)
                found_slot = jnp.where(hit, s, found_slot)
        out_ref[q] = gath[found_lane, found_slot].astype(F32)
    for copy in mail.made:
        copy.wait_send()


def body(self_blk, near, back, interp, redinv, ranks, pivots, neighbors, parent):
    hbm = pl.BlockSpec(memory_space=pl.ANY)
    smem = pl.BlockSpec(memory_space=pltpu.SMEM)
    vmem = pl.BlockSpec(memory_space=pltpu.VMEM)
    blk = (K, K)
    return pl.pallas_call(
        kernel,
        out_shape=jax.ShapeDtypeStruct((BOXES_HERE, K, K), F32),
        in_specs=[hbm] * 5 + [smem, vmem, smem, smem],
        out_specs=vmem,
        scratch_shapes=[
            pltpu.VMEM((BOXES_HERE,) + blk, F32),
            pltpu.VMEM((BOXES_HERE, NBR, PTS, K), BF),
            pltpu.VMEM((BOXES_HERE, NBR, K, PTS), BF),
            pltpu.VMEM((BOXES_HERE, K, PTS), BF),
            pltpu.VMEM((BOXES_HERE, PTS, PTS), BF),
            pltpu.VMEM((BOXES_HERE, PTS, PTS), BF),
            pltpu.VMEM((ENTRIES + 1,) + blk, F32),
            pltpu.VMEM((BOXES_HERE, K), jnp.int32),
            pltpu.SMEM((BOXES_HERE, K), jnp.int32),
            pltpu.VMEM((BOXES_HERE, K), jnp.int32),
            pltpu.VMEM((YS * 2, BOXES_HERE, K), jnp.int32),
            pltpu.SMEM((YS * 2, BOXES_HERE, K), jnp.int32),
            pltpu.VMEM((XS, ZS) + blk, BF),
            pltpu.VMEM((ZS, XS) + blk, BF),
            pltpu.VMEM((2, ZS // 2) + blk, BF),
            pltpu.VMEM((2, ZS) + blk, BF),
            pltpu.VMEM((ZS,) + blk, F32),
            pltpu.VMEM((2, 4) + blk, BF),
            pltpu.VMEM((2, 4) + blk, BF),
            pltpu.VMEM((2, 2, 4, XS // 2) + blk, BF),
            pltpu.VMEM((XS,) + blk, F32),
            pltpu.VMEM((2, 2) + blk, BF),
            pltpu.VMEM((2, 2) + blk, BF),
            pltpu.VMEM((YS * 2, BOXES_HERE) + blk, BF),
            pltpu.SemaphoreType.DMA((9,)),
            pltpu.SemaphoreType.DMA((3,)),
            pltpu.SemaphoreType.DMA((MESSAGES,)),
            pltpu.SemaphoreType.DMA((MESSAGES,)),
        ],
        compiler_params=pltpu.CompilerParams(
            collective_id=0, has_side_effects=True, vmem_limit_bytes=48 << 20),
    )(self_blk, near, back, interp, redinv, ranks, pivots, neighbors, parent)


def solution(mesh):
    wide = ("gx", "gy")
    placed = (
        P(wide, None, None),
        P(wide, None, None, None),
        P(wide, None, None, None),
        P(wide, None, None),
        P(wide, None, None),
        P(wide),
        P(wide, None),
        P(wide, None),
        P(wide),
    )
    return jax.shard_map(
        body, mesh=mesh, in_specs=placed, out_specs=P(wide, None, None), check_vma=False
    )
```

```python
import jax
import jax.numpy as jnp
from jax import lax
from jax.experimental import pallas as pl
from jax.experimental.pallas import tpu as pltpu
from jax.sharding import PartitionSpec as P

BF = jnp.bfloat16
F32 = jnp.float32
MESH = pl.DeviceIdType.MESH
NT = (((1,), (1,)), ((), ()))

XS, ZS, YS = 4, 8, 4
BOXES_HERE, NBR, K, PTS = 2, 14, 128, 512
ENTRIES = BOXES_HERE * NBR
GROUP = 2


class Mail:
    def __init__(self, send_sem, recv_sem):
        self.send_sem, self.recv_sem, self.made = send_sem, recv_sem, []

    def post(self, src, dst, device):
        m = len(self.made)
        copy = pltpu.make_async_remote_copy(
            src_ref=src, dst_ref=dst, send_sem=self.send_sem.at[m],
            recv_sem=self.recv_sem.at[m], device_id=device, device_id_type=MESH)
        copy.start()
        self.made.append(copy)
        return copy


MESSAGES = 96
VMEM_LIMIT = 62 << 20


def make_eliminator(rank, pivot_row, interp, redinv):
    point = lax.broadcasted_iota(jnp.int32, (PTS, K), 0)
    lane = lax.broadcasted_iota(jnp.int32, (PTS, K), 1)
    select_t = jnp.where((point == pivot_row) & (lane < rank), 1.0, 0.0).astype(F32)
    skel_col = jnp.sum(select_t, axis=1, keepdims=True)
    select_t = select_t.astype(BF)
    skel_row = lax.dot_general(jnp.ones((8, K), BF), select_t, NT, preferred_element_type=F32)[0:1]
    living = lax.broadcasted_iota(jnp.int32, (K, PTS), 0) < rank
    coeff = jnp.where(living & (skel_row < 0.5), interp.astype(F32), 0.0).astype(BF)
    through = -lax.dot_general(redinv, coeff, NT, preferred_element_type=F32)
    spread = lax.dot_general(through.astype(BF), select_t, NT, preferred_element_type=F32)
    halfway = jnp.where(skel_row < 0.5, redinv.astype(F32), spread).astype(BF)
    folded = -jnp.dot(coeff, halfway, preferred_element_type=F32)
    placed = jnp.dot(select_t, folded.astype(BF), preferred_element_type=F32)
    return jnp.where(skel_col < 0.5, halfway.astype(F32), placed).astype(BF)


def kernel(self_h, near_h, back_h, interp_h, redinv_h, ranks_s, pivots_v, nbr_s, par_s,
           out_ref,
           self_v, near_v, back_v, interp_v, redinv_v, elim_v, upd_v, tab_v, tab_s,
           own_par, all_par, par_tab,
           out_a, out_b, rxa, sza, rza, acc_a, rzb, sxb, rxb, acc_b, gath,
           load_sem, tab_sem, send_sem, recv_sem):
    gx, gy = lax.axis_index("gx"), lax.axis_index("gy")
    x, z = gx // ZS, gx % ZS
    y, c = gy // 2, gy % 2

    def row(dx, dz):
        return ((x + dx) % XS) * ZS + (z + dz) % ZS

    def lane(dy, dc):
        return ((y + dy) % YS) * 2 + (c + dc) % 2

    zp, zm = (row(0, 1), gy), (row(0, ZS - 1), gy)
    twin = (gx, lane(0, 1))
    lanes = [(gx, lane(dy, dc)) for dy in range(YS) for dc in range(2) if dy or dc]

    barrier = pltpu.get_barrier_semaphore()
    partners = ([(row(dx, 0), gy) for dx in range(1, XS)]
                + [(row(0, dz), gy) for dz in range(1, ZS)] + lanes)
    for device in partners:
        pl.semaphore_signal(barrier, inc=1, device_id=device, device_id_type=MESH)

    loads = []

    def load(src, dst):
        copy = pltpu.make_async_copy(src, dst, load_sem.at[len(loads)])
        copy.start()
        loads.append(copy)
        return copy

    in_i, in_r, in_b, in_n = [], [], [], []
    for b in range(BOXES_HERE):
        in_i.append(load(interp_h.at[b], interp_v.at[b]))
        in_r.append(load(redinv_h.at[b], redinv_v.at[b]))
        in_b.append(load(back_h.at[b], back_v.at[b]))
        in_n.append(load(near_h.at[b], near_v.at[b]))
    in_s = load(self_h, self_v)

    slots = lax.broadcasted_iota(jnp.int32, (1, K), 1)
    for b in range(BOXES_HERE):
        table = jnp.full((1, K), ENTRIES, jnp.int32)
        for n in range(NBR):
            target = nbr_s[b, n]
            slot = (target // (BOXES_HERE * YS * 2)) * BOXES_HERE + target % BOXES_HERE
            table = jnp.where(slots == slot, b * NBR + n, table)
        tab_v[b:b + 1, :] = table
    for b in range(BOXES_HERE):
        own_par[b:b + 1, :] = jnp.full((1, K), par_s[b], jnp.int32)
    tab_copy = pltpu.make_async_copy(tab_v, tab_s, tab_sem.at[0])
    tab_copy.start()
    upd_v[ENTRIES] = jnp.zeros((K, K), F32)

    for b in range(BOXES_HERE):
        in_i[b].wait()
        in_r[b].wait()
        elim_v[b] = make_eliminator(ranks_s[b], pivots_v[b:b + 1, :], interp_v[b], redinv_v[b])
        in_b[b].wait()
        in_n[b].wait()

        def pair(i, carry, b=b):
            rows = back_v[b, pl.ds(2 * i, 2)].reshape(2 * K, PTS)
            lifted = jnp.dot(rows, elim_v[b], preferred_element_type=F32).astype(BF)
            for h in range(2):
                upd_v[b * NBR + 2 * i + h] = jnp.dot(
                    lifted[h * K:(h + 1) * K], near_v[b, 2 * i + h], preferred_element_type=F32)
            return carry

        lax.fori_loop(0, NBR // 2, pair, 0)

    tab_copy.wait()

    def assemble(r, carry):
        kx, p = r // ZS, r % ZS
        kz = lax.select(p % 2 == 0, ZS // 2 + p // 2, ZS // 2 - 1 - p // 2)
        there = ((x + kx) % XS) * ZS + (z + kz) % ZS
        for slot in range(BOXES_HERE):
            s = BOXES_HERE * there + slot
            value = (-(upd_v[tab_s[0, s]] + upd_v[tab_s[1, s]])).astype(BF)
            if slot == 0:
                out_a[kx, p] = value
            else:
                out_b[kz, kx] = value
        return carry

    lax.fori_loop(0, XS * ZS, assemble, 0)

    pl.semaphore_wait(barrier, len(partners))
    mail = Mail(send_sem, recv_sem)

    hop = {}

    def post_b(d, h, k):
        hop[d, h, k] = mail.post(out_b.at[k if d == 0 else ZS - k, h], rzb.at[d, h, k - 1],
                                 zp if d == 0 else zm)

    def pass_b(d, h, k):
        hop[d, h, k + 1].wait_recv()
        t = k if d == 0 else ZS - k
        out_b[t, h] = out_b[t, h] + rzb[d, h, k]
        post_b(d, h, k)

    long_way = [(0, 0), (1, 2), (0, 1), (1, 3)]
    short_way = [(0, 2), (1, 0), (0, 3), (1, 1)]

    cross = {}

    def post_a(g):
        span = pl.ds(g * GROUP, GROUP)
        for kx in (2, 1, 3):
            cross[g, kx] = mail.post(out_a.at[kx, span], rxa.at[kx - 1, span], (row(kx, 0), gy))

    for d, h in long_way:
        post_b(d, h, 4)
    post_a(0)
    for d, h in short_way:
        post_b(d, h, 3)
    for g in range(1, ZS // GROUP):
        post_a(g)

    own_copy = pltpu.make_async_copy(own_par, all_par.at[gy], tab_sem.at[1])
    own_copy.start()
    par_mail = [mail.post(own_par, all_par.at[gy], device) for device in lanes]

    down = {}

    def settle_a(g):
        for kx in (1, 3, 2):
            cross[g, kx].wait_recv()
        for p in range(g * GROUP, (g + 1) * GROUP):
            total = (out_a[0, p].astype(F32) + rxa[0, p].astype(F32)
                     + rxa[1, p].astype(F32) + rxa[2, p].astype(F32))
            kz = ZS // 2 + p // 2 if p % 2 == 0 else ZS // 2 - 1 - p // 2
            if kz:
                sza[p] = total.astype(BF)
                down[p] = mail.post(sza.at[p], rza.at[p], (row(0, kz), gy))
            else:
                acc_a[...] = total

    for d, h in long_way:
        pass_b(d, h, 3)
    for d, h in short_way:
        pass_b(d, h, 2)
    settle_a(0)
    for d, h in long_way:
        pass_b(d, h, 2)
    settle_a(1)
    for d, h in short_way:
        pass_b(d, h, 1)
    settle_a(2)
    for d, h in long_way:
        pass_b(d, h, 1)
    settle_a(3)

    side = {}
    for h in (2, 1, 3, 0):
        for d in range(2):
            hop[d, h, 1].wait_recv()
        total = out_b[0, h].astype(F32) + rzb[0, h, 0].astype(F32) + rzb[1, h, 0].astype(F32)
        if h:
            sxb[h - 1] = total.astype(BF)
            side[h] = mail.post(sxb.at[h - 1], rxb.at[h - 1], (row(h, 0), gy))
        else:
            acc_b[...] = total

    in_s.wait()
    j = lax.broadcasted_iota(jnp.int32, (K, K), 0)
    l = lax.broadcasted_iota(jnp.int32, (K, K), 1)
    away = [lane(dy, 0) for dy in range(YS)]

    def finish(slot, total):
        rank = ranks_s[slot]
        merged = jnp.where((j < rank) & (l < rank), self_v[slot] + total, 0.0)
        gath[gy, slot] = merged.astype(BF)
        return [mail.post(gath.at[gy, slot], gath.at[gy, slot], device)
                for device in ((gx, away[2]), (gx, away[1]), (gx, away[3]), twin)]

    def forward(slot, sent):
        got = [sent[3]]
        for copy, source in ((sent[1], away[3]), (sent[2], away[1]), (sent[0], away[2])):
            copy.wait_recv()
            got.append(mail.post(gath.at[source, slot], gath.at[source, slot], twin))
        return got

    total = acc_a[...]
    for p in range(ZS - 1):
        down[p].wait_recv()
        total = total + rza[p].astype(F32)
    sent_a = finish(0, total)

    total = acc_b[...]
    for h in (1, 3, 2):
        side[h].wait_recv()
        total = total + rxb[h - 1].astype(F32)
    sent_b = finish(1, total)

    own_copy.wait()
    for copy in par_mail:
        copy.wait_recv()
    par_copy = pltpu.make_async_copy(all_par, par_tab, tab_sem.at[2])
    par_copy.start()

    got = forward(0, sent_a)
    got += forward(1, sent_b)
    par_copy.wait()

    first_row = gx * (YS * 2 * BOXES_HERE) + gy * BOXES_HERE
    found = []
    for q in range(BOXES_HERE):
        found_lane, found_slot = jnp.int32(0), jnp.int32(0)
        for k in range(YS * 2):
            for s in range(BOXES_HERE):
                hit = par_tab[k, s, 0] == first_row + q
                found_lane = jnp.where(hit, k, found_lane)
                found_slot = jnp.where(hit, s, found_slot)
        found.append((found_lane, found_slot))
    for copy in got:
        copy.wait_recv()
    for q in range(BOXES_HERE):
        out_ref[q] = gath[found[q][0], found[q][1]].astype(F32)
    for copy in mail.made:
        copy.wait_send()


def body(self_blk, near, back, interp, redinv, ranks, pivots, neighbors, parent):
    hbm = pl.BlockSpec(memory_space=pltpu.HBM)
    smem = pl.BlockSpec(memory_space=pltpu.SMEM)
    vmem = pl.BlockSpec(memory_space=pltpu.VMEM)
    blk = (K, K)
    return pl.pallas_call(
        kernel,
        out_shape=jax.ShapeDtypeStruct((BOXES_HERE, K, K), F32),
        in_specs=[hbm] * 5 + [smem, vmem, smem, smem],
        out_specs=vmem,
        scratch_shapes=[
            pltpu.VMEM((BOXES_HERE,) + blk, F32),
            pltpu.VMEM((BOXES_HERE, NBR, PTS, K), BF),
            pltpu.VMEM((BOXES_HERE, NBR, K, PTS), BF),
            pltpu.VMEM((BOXES_HERE, K, PTS), BF),
            pltpu.VMEM((BOXES_HERE, PTS, PTS), BF),
            pltpu.VMEM((BOXES_HERE, PTS, PTS), BF),
            pltpu.VMEM((ENTRIES + 1,) + blk, F32),
            pltpu.VMEM((BOXES_HERE, K), jnp.int32),
            pltpu.SMEM((BOXES_HERE, K), jnp.int32),
            pltpu.VMEM((BOXES_HERE, K), jnp.int32),
            pltpu.VMEM((YS * 2, BOXES_HERE, K), jnp.int32),
            pltpu.SMEM((YS * 2, BOXES_HERE, K), jnp.int32),
            pltpu.VMEM((XS, ZS) + blk, BF),
            pltpu.VMEM((ZS, XS) + blk, BF),
            pltpu.VMEM((XS - 1, ZS) + blk, BF),
            pltpu.VMEM((ZS - 1,) + blk, BF),
            pltpu.VMEM((ZS - 1,) + blk, BF),
            pltpu.VMEM(blk, F32),
            pltpu.VMEM((2, XS, ZS // 2) + blk, BF),
            pltpu.VMEM((XS - 1,) + blk, BF),
            pltpu.VMEM((XS - 1,) + blk, BF),
            pltpu.VMEM(blk, F32),
            pltpu.VMEM((YS * 2, BOXES_HERE) + blk, BF),
            pltpu.SemaphoreType.DMA((9,)),
            pltpu.SemaphoreType.DMA((3,)),
            pltpu.SemaphoreType.DMA((MESSAGES,)),
            pltpu.SemaphoreType.DMA((MESSAGES,)),
        ],
        compiler_params=pltpu.CompilerParams(
            collective_id=0, has_side_effects=True, vmem_limit_bytes=VMEM_LIMIT),
    )(self_blk, near, back, interp, redinv, ranks, pivots, neighbors, parent)


def solution(mesh):
    wide = ("gx", "gy")
    placed = (
        P(wide, None, None),
        P(wide, None, None, None),
        P(wide, None, None, None),
        P(wide, None, None),
        P(wide, None, None),
        P(wide),
        P(wide, None),
        P(wide, None),
        P(wide),
    )
    return jax.shard_map(
        body, mesh=mesh, in_specs=placed, out_specs=P(wide, None, None), check_vma=False
    )
```

```python
import jax
import jax.numpy as jnp
from jax import lax
from jax.experimental import pallas as pl
from jax.experimental.pallas import tpu as pltpu
from jax.sharding import PartitionSpec as P

BF = jnp.bfloat16
F32 = jnp.float32
MESH = pl.DeviceIdType.MESH
NT = (((1,), (1,)), ((), ()))

XS, ZS, YS = 4, 8, 4
BOXES_HERE, NBR, K, PTS = 2, 14, 128, 512
ENTRIES = BOXES_HERE * NBR
GROUP = 2
RB = 64
RA = K - RB
STEP = 7


class Mail:
    def __init__(self, send_sem, recv_sem):
        self.send_sem, self.recv_sem, self.made = send_sem, recv_sem, []

    def post(self, src, dst, device):
        m = len(self.made)
        copy = pltpu.make_async_remote_copy(
            src_ref=src, dst_ref=dst, send_sem=self.send_sem.at[m],
            recv_sem=self.recv_sem.at[m], device_id=device, device_id_type=MESH)
        copy.start()
        self.made.append(copy)
        return copy


MESSAGES = 96
VMEM_LIMIT = 62 << 20


def make_eliminator(rank, pivot_row, interp, redinv):
    point = lax.broadcasted_iota(jnp.int32, (PTS, K), 0)
    lane = lax.broadcasted_iota(jnp.int32, (PTS, K), 1)
    select_t = jnp.where((point == pivot_row) & (lane < rank), 1.0, 0.0).astype(F32)
    drop_col = (jnp.sum(select_t, axis=1, keepdims=True) - 1.0).astype(BF)
    select_t = select_t.astype(BF)
    taken = lax.dot_general(jnp.ones((8, K), BF), select_t, NT, preferred_element_type=F32)
    keep_row = (1.0 - taken[0:1]).astype(BF)
    living = jnp.where(lax.broadcasted_iota(jnp.int32, (K, 1), 0) < rank, 1.0, 0.0).astype(BF)
    coeff = interp * living * keep_row
    through = -lax.dot_general(redinv, coeff, NT, preferred_element_type=F32)
    spread = lax.dot_general(through.astype(BF), select_t, NT, preferred_element_type=F32)
    halfway = redinv * keep_row + spread.astype(BF)
    folded = jnp.dot(coeff, halfway, preferred_element_type=F32)
    placed = jnp.dot(select_t, folded.astype(BF), preferred_element_type=F32)
    return halfway * drop_col + placed.astype(BF)


def kernel(self_h, near_h, back_h, interp_h, redinv_h, ranks_h, pivots_h, nbr_h, par_h,
           out_ref,
           self_v, near_v, back_v, interp_v, redinv_v, elim_v, upd_a, upd_b, tab_v, tab_s,
           own_par, all_par, par_tab, ranks_s, pivots_v, nbr_s, par_s,
           out_a, out_b, rxa, sza, rza, acc_a, rzb, sxb, rxb, acc_b, gath_a, gath_b,
           load_sem, tab_sem, send_sem, recv_sem):
    gx, gy = lax.axis_index("gx"), lax.axis_index("gy")
    x, z = gx // ZS, gx % ZS
    y, c = gy // 2, gy % 2

    def row(dx, dz):
        return ((x + dx) % XS) * ZS + (z + dz) % ZS

    def lane(dy, dc):
        return ((y + dy) % YS) * 2 + (c + dc) % 2

    twin = (gx, lane(0, 1))
    lanes = [(gx, lane(dy, dc)) for dy in range(YS) for dc in range(2) if dy or dc]

    barrier = pltpu.get_barrier_semaphore()
    partners = ([(row(dx, 0), gy) for dx in range(1, XS)]
                + [(row(0, dz), gy) for dz in range(1, ZS)] + lanes)
    for device in partners:
        pl.semaphore_signal(barrier, inc=1, device_id=device, device_id_type=MESH)

    loads = []

    def load(src, dst):
        copy = pltpu.make_async_copy(src, dst, load_sem.at[len(loads)])
        copy.start()
        loads.append(copy)
        return copy

    in_small = [load(ranks_h, ranks_s), load(pivots_h, pivots_v), load(nbr_h, nbr_s),
                load(par_h, par_s)]
    in_i = [load(interp_h.at[b], interp_v.at[b]) for b in range(BOXES_HERE)]
    in_r = [load(redinv_h.at[b], redinv_v.at[b]) for b in range(BOXES_HERE)]
    in_low, in_n = [], []

    def load_box(b):
        in_low.append(load(back_h.at[b, :, pl.ds(0, RB)], back_v.at[b, :, pl.ds(0, RB)]))
        in_n.append(load(near_h.at[b], near_v.at[b]))


    in_small[0].wait()
    in_small[1].wait()
    upd_a[ENTRIES] = jnp.zeros((RA, K), F32)
    upd_b[ENTRIES] = jnp.zeros((RB, K), F32)

    for b in range(BOXES_HERE):
        in_i[b].wait()
        in_r[b].wait()
        load_box(b)
        elim_v[b] = make_eliminator(ranks_s[b], pivots_v[b:b + 1, :], interp_v[b], redinv_v[b])
    in_high = [load(back_h.at[b, :, pl.ds(RB, RA)], back_v.at[b, :, pl.ds(RB, RA)])
               for b in range(BOXES_HERE)]
    in_s = load(self_h, self_v)

    in_small[2].wait()
    in_small[3].wait()
    slots = lax.broadcasted_iota(jnp.int32, (1, K), 1)
    for b in range(BOXES_HERE):
        table = jnp.full((1, K), ENTRIES, jnp.int32)
        for n in range(NBR):
            target = nbr_s[b, n]
            slot = (target // (BOXES_HERE * YS * 2)) * BOXES_HERE + target % BOXES_HERE
            table = jnp.where(slots == slot, b * NBR + n, table)
        tab_v[b:b + 1, :] = table
    for b in range(BOXES_HERE):
        own_par[b:b + 1, :] = jnp.full((1, K), par_s[b], jnp.int32)
    tab_copy = pltpu.make_async_copy(tab_v, tab_s, tab_sem.at[0])
    tab_copy.start()
    own_copy = pltpu.make_async_copy(own_par, all_par.at[gy], tab_sem.at[1])
    own_copy.start()
    def products(upd, first, rows, needs):
        for b in range(BOXES_HERE):
            for copies in needs:
                copies[b].wait()

            def step(i, carry, b=b):
                wide = back_v[b, pl.ds(STEP * i, STEP), first:first + rows].reshape(STEP * rows, PTS)
                lifted = jnp.dot(wide, elim_v[b], preferred_element_type=F32).astype(BF)
                for h in range(STEP):
                    upd[b * NBR + STEP * i + h] = jnp.dot(
                        lifted[h * rows:(h + 1) * rows], near_v[b, STEP * i + h],
                        preferred_element_type=F32)
                return carry

            lax.fori_loop(0, NBR // STEP, step, 0)

    def order(p):
        return ZS // 2 + p // 2 if p % 2 == 0 else ZS // 2 - 1 - p // 2

    def gathered(upd, kx, kz):
        there = ((x + kx) % XS) * ZS + (z + kz) % ZS
        s = BOXES_HERE * there
        return [(upd[tab_s[0, s + q]] + upd[tab_s[1, s + q]]).astype(BF)
                for q in range(BOXES_HERE)]

    def assemble_b(*kzs):
        def one(kx, carry):
            for kz in kzs:
                for q, value in enumerate(gathered(upd_b, kx, kz)):
                    out_b[kz, kx, q] = value
            return carry

        lax.fori_loop(0, XS, one, 0)

    def assemble_a(g):
        def one(kx, carry):
            for p in range(g * GROUP, (g + 1) * GROUP):
                for q, value in enumerate(gathered(upd_a, kx, order(p))):
                    out_a[kx, p, q] = value
            return carry

        lax.fori_loop(0, XS, one, 0)

    mail = Mail(send_sem, recv_sem)

    hop = {}
    long_way = [(0, 0), (1, 2), (0, 1), (1, 3)]
    short_way = [(0, 2), (1, 0), (0, 3), (1, 1)]
    ways = [pair for both in zip(long_way, short_way) for pair in both]

    def toward(d, k):
        return k if d == 0 else ZS - k

    def post_b(d, h, k, links):
        hop[d, h, k] = mail.post(out_b.at[toward(d, k), h], rzb.at[d, h, k - 1],
                                 (row(0, toward(d, links)), gy))

    def pass_b(d, h, k):
        total = out_b[toward(d, k), h].astype(F32)
        if k == 2 and (d, h) in long_way:
            hop[d, h, 4].wait_recv()
            total = total + rzb[d, h, 3].astype(F32)
        hop[d, h, k + 1].wait_recv()
        out_b[toward(d, k), h] = (total + rzb[d, h, k].astype(F32)).astype(BF)
        post_b(d, h, k, 1)

    cross = {}

    def post_a(g):
        span = pl.ds(g * GROUP, GROUP)
        for kx in (2, 1, 3):
            cross[g, kx] = mail.post(out_a.at[kx, span], rxa.at[kx - 1, span], (row(kx, 0), gy))

    products(upd_b, 0, RB, (in_low, in_n))
    tab_copy.wait()
    assemble_b(4)
    pl.semaphore_wait(barrier, len(partners))
    for d, h in long_way:
        post_b(d, h, 4, 2)
    assemble_b(3, 5)
    for d, h in ways:
        post_b(d, h, 3, 1)
    assemble_b(2, 6)
    assemble_b(1, 7, 0)

    products(upd_a, RB, RA, (in_high,))
    for g in range(ZS // GROUP):
        assemble_a(g)
        post_a(g)
    par_mail = [mail.post(own_par, all_par.at[gy], device) for device in lanes]

    down = {}

    def settle_a(g):
        for kx in (1, 3, 2):
            cross[g, kx].wait_recv()
        for p in range(g * GROUP, (g + 1) * GROUP):
            total = (out_a[0, p].astype(F32) + rxa[0, p].astype(F32)
                     + rxa[1, p].astype(F32) + rxa[2, p].astype(F32))
            kz = order(p)
            if kz:
                sza[p] = total.astype(BF)
                down[p] = mail.post(sza.at[p], rza.at[p], (row(0, kz), gy))
            else:
                acc_a[...] = total

    for d, h in ways:
        pass_b(d, h, 2)
    for d, h in ways:
        pass_b(d, h, 1)
    settle_a(0)
    side = {}
    for h in (2, 1, 3, 0):
        for d in range(2):
            hop[d, h, 1].wait_recv()
        total = out_b[0, h].astype(F32) + rzb[0, h, 0].astype(F32) + rzb[1, h, 0].astype(F32)
        if h:
            sxb[h - 1] = total.astype(BF)
            side[h] = mail.post(sxb.at[h - 1], rxb.at[h - 1], (row(h, 0), gy))
        else:
            acc_b[...] = total
    settle_a(1)
    settle_a(2)
    settle_a(3)

    in_s.wait()
    away = [lane(dy, 0) for dy in range(YS)]

    def finish(gath, first, rows, total):
        j = lax.broadcasted_iota(jnp.int32, (rows, K), 0) + first
        l = lax.broadcasted_iota(jnp.int32, (rows, K), 1)
        for q in range(BOXES_HERE):
            rank = ranks_s[q]
            merged = jnp.where((j < rank) & (l < rank), self_v[q, first:first + rows] + total[q], 0.0)
            gath[gy, q] = merged.astype(BF)
        return [mail.post(gath.at[gy], gath.at[gy], device)
                for device in ((gx, away[2]), (gx, away[1]), (gx, away[3]), twin)]

    def forward(gath, sent):
        got = [sent[3]]
        for copy, source in ((sent[1], away[3]), (sent[2], away[1]), (sent[0], away[2])):
            copy.wait_recv()
            got.append(mail.post(gath.at[source], gath.at[source], twin))
        return got

    total = acc_b[...]
    for h in (1, 3, 2):
        side[h].wait_recv()
        total = total + rxb[h - 1].astype(F32)
    sent_b = finish(gath_b, 0, RB, total)

    total = acc_a[...]
    for p in range(ZS - 1):
        down[p].wait_recv()
        total = total + rza[p].astype(F32)
    sent_a = finish(gath_a, RB, RA, total)

    own_copy.wait()
    for copy in par_mail:
        copy.wait_recv()
    par_copy = pltpu.make_async_copy(all_par, par_tab, tab_sem.at[2])
    par_copy.start()

    got = forward(gath_b, sent_b)
    got += forward(gath_a, sent_a)
    par_copy.wait()

    first_row = gx * (YS * 2 * BOXES_HERE) + gy * BOXES_HERE
    found = []
    for q in range(BOXES_HERE):
        found_lane, found_slot = jnp.int32(0), jnp.int32(0)
        for k in range(YS * 2):
            for s in range(BOXES_HERE):
                hit = par_tab[k, s, 0] == first_row + q
                found_lane = jnp.where(hit, k, found_lane)
                found_slot = jnp.where(hit, s, found_slot)
        found.append((found_lane, found_slot))
    for copy in got:
        copy.wait_recv()
    for q in range(BOXES_HERE):
        out_ref[q, 0:RB] = gath_b[found[q][0], found[q][1]]
        out_ref[q, RB:K] = gath_a[found[q][0], found[q][1]]
    for copy in mail.made:
        copy.wait_send()


def body(self_blk, near, back, interp, redinv, ranks, pivots, neighbors, parent):
    hbm = pl.BlockSpec(memory_space=pl.ANY)
    a_blk, b_blk = (BOXES_HERE, RA, K), (BOXES_HERE, RB, K)
    rows = pl.pallas_call(
        kernel,
        out_shape=jax.ShapeDtypeStruct((BOXES_HERE, K, K), BF),
        in_specs=[hbm] * 9,
        out_specs=pl.BlockSpec(memory_space=pltpu.VMEM),
        scratch_shapes=[
            pltpu.VMEM((BOXES_HERE, K, K), F32),
            pltpu.VMEM((BOXES_HERE, NBR, PTS, K), BF),
            pltpu.VMEM((BOXES_HERE, NBR, K, PTS), BF),
            pltpu.VMEM((BOXES_HERE, K, PTS), BF),
            pltpu.VMEM((BOXES_HERE, PTS, PTS), BF),
            pltpu.VMEM((BOXES_HERE, PTS, PTS), BF),
            pltpu.VMEM((ENTRIES + 1, RA, K), F32),
            pltpu.VMEM((ENTRIES + 1, RB, K), F32),
            pltpu.VMEM((BOXES_HERE, K), jnp.int32),
            pltpu.SMEM((BOXES_HERE, K), jnp.int32),
            pltpu.VMEM((BOXES_HERE, K), jnp.int32),
            pltpu.VMEM((YS * 2, BOXES_HERE, K), jnp.int32),
            pltpu.SMEM((YS * 2, BOXES_HERE, K), jnp.int32),
            pltpu.SMEM((BOXES_HERE,), jnp.int32),
            pltpu.VMEM((BOXES_HERE, K), jnp.int32),
            pltpu.SMEM((BOXES_HERE, NBR), jnp.int32),
            pltpu.SMEM((BOXES_HERE,), jnp.int32),
            pltpu.VMEM((XS, ZS) + a_blk, BF),
            pltpu.VMEM((ZS, XS) + b_blk, BF),
            pltpu.VMEM((XS - 1, ZS) + a_blk, BF),
            pltpu.VMEM((ZS - 1,) + a_blk, BF),
            pltpu.VMEM((ZS - 1,) + a_blk, BF),
            pltpu.VMEM(a_blk, F32),
            pltpu.VMEM((2, XS, ZS // 2) + b_blk, BF),
            pltpu.VMEM((XS - 1,) + b_blk, BF),
            pltpu.VMEM((XS - 1,) + b_blk, BF),
            pltpu.VMEM(b_blk, F32),
            pltpu.VMEM((YS * 2,) + a_blk, BF),
            pltpu.VMEM((YS * 2,) + b_blk, BF),
            pltpu.SemaphoreType.DMA((15,)),
            pltpu.SemaphoreType.DMA((3,)),
            pltpu.SemaphoreType.DMA((MESSAGES,)),
            pltpu.SemaphoreType.DMA((MESSAGES,)),
        ],
        compiler_params=pltpu.CompilerParams(
            collective_id=0, has_side_effects=True, vmem_limit_bytes=VMEM_LIMIT),
    )(self_blk, near, back, interp, redinv, ranks, pivots, neighbors, parent)
    return rows.astype(F32)


def solution(mesh):
    wide = ("gx", "gy")
    placed = (
        P(wide, None, None),
        P(wide, None, None, None),
        P(wide, None, None, None),
        P(wide, None, None),
        P(wide, None, None),
        P(wide),
        P(wide, None),
        P(wide, None),
        P(wide),
    )
    return jax.shard_map(
        body, mesh=mesh, in_specs=placed, out_specs=P(wide, None, None), check_vma=False
    )
```

```python
import jax
import jax.numpy as jnp
from jax import lax
from jax.experimental import pallas as pl
from jax.experimental.pallas import tpu as pltpu
from jax.sharding import PartitionSpec as P

BF = jnp.bfloat16
F32 = jnp.float32
MESH = pl.DeviceIdType.MESH
NT = (((1,), (1,)), ((), ()))

XS, ZS, YS = 4, 8, 4
BOXES_HERE, NBR, K, PTS = 2, 14, 128, 512
ENTRIES = BOXES_HERE * NBR
GROUP = 2
RB = 64
RA = K - RB


class Mail:
    def __init__(self, send_sem, recv_sem):
        self.send_sem, self.recv_sem, self.made = send_sem, recv_sem, []

    def post(self, src, dst, device):
        m = len(self.made)
        copy = pltpu.make_async_remote_copy(
            src_ref=src, dst_ref=dst, send_sem=self.send_sem.at[m],
            recv_sem=self.recv_sem.at[m], device_id=device, device_id_type=MESH)
        copy.start()
        self.made.append(copy)
        return copy


MESSAGES = 96
VMEM_LIMIT = 62 << 20


def select_points(rank, pivot_row, interp):
    point = lax.broadcasted_iota(jnp.int32, (PTS, K), 0)
    lane = lax.broadcasted_iota(jnp.int32, (PTS, K), 1)
    select_t = jnp.where((point == pivot_row) & (lane < rank), 1.0, 0.0).astype(F32)
    drop_col = (jnp.sum(select_t, axis=1, keepdims=True) - 1.0).astype(BF)
    select_t = select_t.astype(BF)
    taken = lax.dot_general(jnp.ones((8, K), BF), select_t, NT, preferred_element_type=F32)
    keep_row = (1.0 - taken[0:1]).astype(BF)
    living = jnp.where(lax.broadcasted_iota(jnp.int32, (K, 1), 0) < rank, 1.0, 0.0).astype(BF)
    return select_t, drop_col, keep_row, interp * living * keep_row


def make_eliminators(ranks_s, pivots_v, interp_v, redinv_v, elim_v):
    boxes = range(BOXES_HERE)
    select_t, drop_col, keep_row, coeff = zip(*[
        select_points(ranks_s[b], pivots_v[b:b + 1, :], interp_v[b]) for b in boxes])
    through = [(-lax.dot_general(redinv_v[b], coeff[b], NT, preferred_element_type=F32)).astype(BF)
               for b in boxes]
    spread = [lax.dot_general(through[b], select_t[b], NT, preferred_element_type=F32).astype(BF)
              for b in boxes]
    halfway = [redinv_v[b] * keep_row[b] + spread[b] for b in boxes]
    folded = [jnp.dot(coeff[b], halfway[b], preferred_element_type=F32).astype(BF) for b in boxes]
    placed = [jnp.dot(select_t[b], folded[b], preferred_element_type=F32).astype(BF) for b in boxes]
    for b in boxes:
        elim_v[b] = halfway[b] * drop_col[b] + placed[b]


def kernel(self_h, near_h, back_h, interp_h, redinv_h, ranks_h, pivots_h, nbr_h, par_h,
           out_ref,
           self_v, near_v, back_v, interp_v, redinv_v, elim_v, upd_a, upd_b, tab_v, tab_s,
           own_par, all_par, par_tab, ranks_s, pivots_v, nbr_s, par_s,
           out_a, out_b, rxa, sza, rza, acc_a, rzb, sxb, rxb, acc_b, gath_a, gath_b,
           load_sem, tab_sem, send_sem, recv_sem):
    gx, gy = lax.axis_index("gx"), lax.axis_index("gy")
    x, z = gx // ZS, gx % ZS
    y, c = gy // 2, gy % 2

    def row(dx, dz):
        return ((x + dx) % XS) * ZS + (z + dz) % ZS

    def lane(dy, dc):
        return ((y + dy) % YS) * 2 + (c + dc) % 2

    twin = (gx, lane(0, 1))
    lanes = [(gx, lane(dy, dc)) for dy in range(YS) for dc in range(2) if dy or dc]

    loads = []

    def load(src, dst):
        copy = pltpu.make_async_copy(src, dst, load_sem.at[len(loads)])
        copy.start()
        loads.append(copy)
        return copy

    in_small = [load(ranks_h, ranks_s), load(pivots_h, pivots_v), load(nbr_h, nbr_s),
                load(par_h, par_s)]
    in_i = [load(interp_h.at[b], interp_v.at[b]) for b in range(BOXES_HERE)]
    in_r = [load(redinv_h.at[b], redinv_v.at[b]) for b in range(BOXES_HERE)]
    barrier = pltpu.get_barrier_semaphore()
    partners = ([(row(dx, 0), gy) for dx in range(1, XS)]
                + [(row(0, dz), gy) for dz in range(1, ZS)] + lanes)
    for device in partners:
        pl.semaphore_signal(barrier, inc=1, device_id=device, device_id_type=MESH)

    in_low, in_n = [], []

    def load_box(b):
        in_low.append(load(back_h.at[b, :, pl.ds(0, RB)], back_v.at[b, :, pl.ds(0, RB)]))
        in_n.append(load(near_h.at[b], near_v.at[b]))


    load_box(0)
    in_small[0].wait()
    in_small[1].wait()
    upd_a[ENTRIES] = jnp.zeros((RA, K), F32)
    upd_b[ENTRIES] = jnp.zeros((RB, K), F32)

    for copy in in_i + in_r:
        copy.wait()
    load_box(1)
    make_eliminators(ranks_s, pivots_v, interp_v, redinv_v, elim_v)
    in_high = [load(back_h.at[b, :, pl.ds(RB, RA)], back_v.at[b, :, pl.ds(RB, RA)])
               for b in range(BOXES_HERE)]
    in_s = load(self_h, self_v)

    in_small[2].wait()
    in_small[3].wait()
    slots = lax.broadcasted_iota(jnp.int32, (1, K), 1)
    for b in range(BOXES_HERE):
        table = jnp.full((1, K), ENTRIES, jnp.int32)
        for n in range(NBR):
            target = nbr_s[b, n]
            slot = (target // (BOXES_HERE * YS * 2)) * BOXES_HERE + target % BOXES_HERE
            table = jnp.where(slots == slot, b * NBR + n, table)
        tab_v[b:b + 1, :] = table
    for b in range(BOXES_HERE):
        own_par[b:b + 1, :] = jnp.full((1, K), par_s[b], jnp.int32)
    tab_copy = pltpu.make_async_copy(tab_v, tab_s, tab_sem.at[0])
    tab_copy.start()
    own_copy = pltpu.make_async_copy(own_par, all_par.at[gy], tab_sem.at[1])
    own_copy.start()
    def products(upd, first, rows, needs):
        for b in range(BOXES_HERE):
            for copies in needs:
                copies[b].wait()

            wide = back_v[b, :, first:first + rows].reshape(NBR * rows, PTS)
            lifted = jnp.dot(wide, elim_v[b], preferred_element_type=F32).astype(BF)
            for n in range(NBR):
                upd[b * NBR + n] = jnp.dot(lifted[n * rows:(n + 1) * rows], near_v[b, n],
                                           preferred_element_type=F32)

    def order(p):
        return ZS // 2 + p // 2 if p % 2 == 0 else ZS // 2 - 1 - p // 2

    def gathered(upd, kx, kz):
        there = ((x + kx) % XS) * ZS + (z + kz) % ZS
        s = BOXES_HERE * there
        return [(upd[tab_s[0, s + q]] + upd[tab_s[1, s + q]]).astype(BF)
                for q in range(BOXES_HERE)]

    def assemble_b(*kzs):
        def one(kx, carry):
            for kz in kzs:
                for q, value in enumerate(gathered(upd_b, kx, kz)):
                    out_b[kz, kx, q] = value
            return carry

        lax.fori_loop(0, XS, one, 0)

    def assemble_a(g):
        def one(kx, carry):
            for p in range(g * GROUP, (g + 1) * GROUP):
                for q, value in enumerate(gathered(upd_a, kx, order(p))):
                    out_a[kx, p, q] = value
            return carry

        lax.fori_loop(0, XS, one, 0)

    mail = Mail(send_sem, recv_sem)

    hop = {}
    long_way = [(0, 0), (1, 2), (0, 1), (1, 3)]
    short_way = [(0, 2), (1, 0), (0, 3), (1, 1)]
    ways = [pair for both in zip(long_way, short_way) for pair in both]

    def toward(d, k):
        return k if d == 0 else ZS - k

    def post_b(d, h, k, links):
        hop[d, h, k] = mail.post(out_b.at[toward(d, k), h], rzb.at[d, h, k - 1],
                                 (row(0, toward(d, links)), gy))

    def pass_b(d, h, k):
        total = out_b[toward(d, k), h].astype(F32)
        if k == 2 and (d, h) in long_way:
            hop[d, h, 4].wait_recv()
            total = total + rzb[d, h, 3].astype(F32)
        hop[d, h, k + 1].wait_recv()
        out_b[toward(d, k), h] = (total + rzb[d, h, k].astype(F32)).astype(BF)
        post_b(d, h, k, 1)

    cross = {}

    def post_a(g):
        span = pl.ds(g * GROUP, GROUP)
        for kx in (2, 1, 3):
            cross[g, kx] = mail.post(out_a.at[kx, span], rxa.at[kx - 1, span], (row(kx, 0), gy))

    products(upd_b, 0, RB, (in_low, in_n))
    tab_copy.wait()
    assemble_b(4)
    pl.semaphore_wait(barrier, len(partners))
    for d, h in long_way:
        post_b(d, h, 4, 2)
    assemble_b(3, 5)
    for d, h in ways:
        post_b(d, h, 3, 1)
    assemble_b(2, 6)
    assemble_b(1, 7, 0)

    products(upd_a, RB, RA, (in_high,))
    for g in range(ZS // GROUP):
        assemble_a(g)
        post_a(g)
    par_mail = [mail.post(own_par, all_par.at[gy], device) for device in lanes]

    down = {}

    def settle_a(g):
        for kx in (1, 3, 2):
            cross[g, kx].wait_recv()
        for p in range(g * GROUP, (g + 1) * GROUP):
            total = (out_a[0, p].astype(F32) + rxa[0, p].astype(F32)
                     + rxa[1, p].astype(F32) + rxa[2, p].astype(F32))
            kz = order(p)
            if kz:
                sza[p] = total.astype(BF)
                down[p] = mail.post(sza.at[p], rza.at[p], (row(0, kz), gy))
            else:
                acc_a[...] = total

    for d, h in ways:
        pass_b(d, h, 2)
    for d, h in ways:
        pass_b(d, h, 1)
    settle_a(0)
    side = {}
    for h in (2, 1, 3, 0):
        for d in range(2):
            hop[d, h, 1].wait_recv()
        total = out_b[0, h].astype(F32) + rzb[0, h, 0].astype(F32) + rzb[1, h, 0].astype(F32)
        if h:
            sxb[h - 1] = total.astype(BF)
            side[h] = mail.post(sxb.at[h - 1], rxb.at[h - 1], (row(h, 0), gy))
        else:
            acc_b[...] = total
    settle_a(1)
    settle_a(2)
    settle_a(3)

    in_s.wait()
    away = [lane(dy, 0) for dy in range(YS)]

    def finish(gath, first, rows, total):
        j = lax.broadcasted_iota(jnp.int32, (rows, K), 0) + first
        l = lax.broadcasted_iota(jnp.int32, (rows, K), 1)
        for q in range(BOXES_HERE):
            rank = ranks_s[q]
            merged = jnp.where((j < rank) & (l < rank), self_v[q, first:first + rows] + total[q], 0.0)
            gath[gy, q] = merged.astype(BF)
        return [mail.post(gath.at[gy], gath.at[gy], device)
                for device in ((gx, away[2]), (gx, away[1]), (gx, away[3]), twin)]

    def forward(gath, sent):
        got = [sent[3]]
        for copy, source in ((sent[1], away[3]), (sent[2], away[1]), (sent[0], away[2])):
            copy.wait_recv()
            got.append(mail.post(gath.at[source], gath.at[source], twin))
        return got

    total = acc_b[...]
    for h in (1, 3, 2):
        side[h].wait_recv()
        total = total + rxb[h - 1].astype(F32)
    sent_b = finish(gath_b, 0, RB, total)

    total = acc_a[...]
    for p in range(ZS - 1):
        down[p].wait_recv()
        total = total + rza[p].astype(F32)
    sent_a = finish(gath_a, RB, RA, total)

    own_copy.wait()
    for copy in par_mail:
        copy.wait_recv()
    par_copy = pltpu.make_async_copy(all_par, par_tab, tab_sem.at[2])
    par_copy.start()

    got = forward(gath_b, sent_b)
    got += forward(gath_a, sent_a)
    par_copy.wait()

    first_row = gx * (YS * 2 * BOXES_HERE) + gy * BOXES_HERE
    found = []
    for q in range(BOXES_HERE):
        found_lane, found_slot = jnp.int32(0), jnp.int32(0)
        for k in range(YS * 2):
            for s in range(BOXES_HERE):
                hit = par_tab[k, s, 0] == first_row + q
                found_lane = jnp.where(hit, k, found_lane)
                found_slot = jnp.where(hit, s, found_slot)
        found.append((found_lane, found_slot))
    for copy in got:
        copy.wait_recv()
    for q in range(BOXES_HERE):
        out_ref[q, 0:RB] = gath_b[found[q][0], found[q][1]]
        out_ref[q, RB:K] = gath_a[found[q][0], found[q][1]]
    for copy in mail.made:
        copy.wait_send()


def body(self_blk, near, back, interp, redinv, ranks, pivots, neighbors, parent):
    hbm = pl.BlockSpec(memory_space=pl.ANY)
    a_blk, b_blk = (BOXES_HERE, RA, K), (BOXES_HERE, RB, K)
    rows = pl.pallas_call(
        kernel,
        out_shape=jax.ShapeDtypeStruct((BOXES_HERE, K, K), BF),
        in_specs=[hbm] * 9,
        out_specs=pl.BlockSpec(memory_space=pltpu.VMEM),
        scratch_shapes=[
            pltpu.VMEM((BOXES_HERE, K, K), F32),
            pltpu.VMEM((BOXES_HERE, NBR, PTS, K), BF),
            pltpu.VMEM((BOXES_HERE, NBR, K, PTS), BF),
            pltpu.VMEM((BOXES_HERE, K, PTS), BF),
            pltpu.VMEM((BOXES_HERE, PTS, PTS), BF),
            pltpu.VMEM((BOXES_HERE, PTS, PTS), BF),
            pltpu.VMEM((ENTRIES + 1, RA, K), F32),
            pltpu.VMEM((ENTRIES + 1, RB, K), F32),
            pltpu.VMEM((BOXES_HERE, K), jnp.int32),
            pltpu.SMEM((BOXES_HERE, K), jnp.int32),
            pltpu.VMEM((BOXES_HERE, K), jnp.int32),
            pltpu.VMEM((YS * 2, BOXES_HERE, K), jnp.int32),
            pltpu.SMEM((YS * 2, BOXES_HERE, K), jnp.int32),
            pltpu.SMEM((BOXES_HERE,), jnp.int32),
            pltpu.VMEM((BOXES_HERE, K), jnp.int32),
            pltpu.SMEM((BOXES_HERE, NBR), jnp.int32),
            pltpu.SMEM((BOXES_HERE,), jnp.int32),
            pltpu.VMEM((XS, ZS) + a_blk, BF),
            pltpu.VMEM((ZS, XS) + b_blk, BF),
            pltpu.VMEM((XS - 1, ZS) + a_blk, BF),
            pltpu.VMEM((ZS - 1,) + a_blk, BF),
            pltpu.VMEM((ZS - 1,) + a_blk, BF),
            pltpu.VMEM(a_blk, F32),
            pltpu.VMEM((2, XS, ZS // 2) + b_blk, BF),
            pltpu.VMEM((XS - 1,) + b_blk, BF),
            pltpu.VMEM((XS - 1,) + b_blk, BF),
            pltpu.VMEM(b_blk, F32),
            pltpu.VMEM((YS * 2,) + a_blk, BF),
            pltpu.VMEM((YS * 2,) + b_blk, BF),
            pltpu.SemaphoreType.DMA((15,)),
            pltpu.SemaphoreType.DMA((3,)),
            pltpu.SemaphoreType.DMA((MESSAGES,)),
            pltpu.SemaphoreType.DMA((MESSAGES,)),
        ],
        compiler_params=pltpu.CompilerParams(
            collective_id=0, has_side_effects=True, vmem_limit_bytes=VMEM_LIMIT),
    )(self_blk, near, back, interp, redinv, ranks, pivots, neighbors, parent)
    return rows.astype(F32)


def solution(mesh):
    wide = ("gx", "gy")
    placed = (
        P(wide, None, None),
        P(wide, None, None, None),
        P(wide, None, None, None),
        P(wide, None, None),
        P(wide, None, None),
        P(wide),
        P(wide, None),
        P(wide, None),
        P(wide),
    )
    return jax.shard_map(
        body, mesh=mesh, in_specs=placed, out_specs=P(wide, None, None), check_vma=False
    )
```

```python
import jax
import jax.numpy as jnp
from jax import lax
from jax.experimental import pallas as pl
from jax.experimental.pallas import tpu as pltpu
from jax.sharding import PartitionSpec as P

BF = jnp.bfloat16
F32 = jnp.float32
MESH = pl.DeviceIdType.MESH
NT = (((1,), (1,)), ((), ()))

XS, ZS, YS = 4, 8, 4
BOXES_HERE, NBR, K, PTS = 2, 14, 128, 512
ENTRIES = BOXES_HERE * NBR
GROUP = 2
RB = 64
RA = K - RB


class Mail:
    def __init__(self, send_sem, recv_sem):
        self.send_sem, self.recv_sem, self.made = send_sem, recv_sem, []

    def post(self, src, dst, device):
        m = len(self.made)
        copy = pltpu.make_async_remote_copy(
            src_ref=src, dst_ref=dst, send_sem=self.send_sem.at[m],
            recv_sem=self.recv_sem.at[m], device_id=device, device_id_type=MESH)
        copy.start()
        self.made.append(copy)
        return copy


MESSAGES = 96
VMEM_LIMIT = 62 << 20


def select_points(rank, pivot_row, interp):
    point = lax.broadcasted_iota(jnp.int32, (PTS, K), 0)
    lane = lax.broadcasted_iota(jnp.int32, (PTS, K), 1)
    select_t = jnp.where((point == pivot_row) & (lane < rank), 1.0, 0.0).astype(F32)
    drop_col = (jnp.sum(select_t, axis=1, keepdims=True) - 1.0).astype(BF)
    select_t = select_t.astype(BF)
    taken = lax.dot_general(jnp.ones((8, K), BF), select_t, NT, preferred_element_type=F32)
    keep_row = (1.0 - taken[0:1]).astype(BF)
    living = jnp.where(lax.broadcasted_iota(jnp.int32, (K, 1), 0) < rank, 1.0, 0.0).astype(BF)
    return select_t, drop_col, keep_row, interp * living * keep_row


def make_eliminators(ranks_s, pivots_v, interp_v, redinv_v, elim_v):
    boxes = range(BOXES_HERE)
    select_t, drop_col, keep_row, coeff = zip(*[
        select_points(ranks_s[b], pivots_v[b:b + 1, :], interp_v[b]) for b in boxes])
    through = [(-lax.dot_general(redinv_v[b], coeff[b], NT, preferred_element_type=F32)).astype(BF)
               for b in boxes]
    spread = [lax.dot_general(through[b], select_t[b], NT, preferred_element_type=F32).astype(BF)
              for b in boxes]
    halfway = [redinv_v[b] * keep_row[b] + spread[b] for b in boxes]
    folded = [jnp.dot(coeff[b], halfway[b], preferred_element_type=F32).astype(BF) for b in boxes]
    placed = [jnp.dot(select_t[b], folded[b], preferred_element_type=F32).astype(BF) for b in boxes]
    for b in boxes:
        elim_v[b] = halfway[b] * drop_col[b] + placed[b]


def kernel(self_h, near_h, back_h, interp_h, redinv_h, ranks_h, pivots_h, nbr_h, par_h,
           out_ref,
           self_v, near_v, back_v, interp_v, redinv_v, elim_v, upd_a, upd_b, tab_v, tab_s,
           own_par, all_par, par_tab, ranks_s, pivots_v, nbr_s, par_s,
           out_a, out_b, rxa, sza, rza, acc_a, rzb, sxb, rxb, acc_b, gath_a, gath_b,
           load_sem, tab_sem, send_sem, recv_sem):
    gx, gy = lax.axis_index("gx"), lax.axis_index("gy")
    x, z = gx // ZS, gx % ZS
    y, c = gy // 2, gy % 2

    def row(dx, dz):
        return ((x + dx) % XS) * ZS + (z + dz) % ZS

    def lane(dy, dc):
        return ((y + dy) % YS) * 2 + (c + dc) % 2

    twin = (gx, lane(0, 1))
    lanes = [(gx, lane(dy, dc)) for dy in range(YS) for dc in range(2) if dy or dc]

    loads = []

    def load(src, dst):
        copy = pltpu.make_async_copy(src, dst, load_sem.at[len(loads)])
        copy.start()
        loads.append(copy)
        return copy

    in_small = [load(ranks_h, ranks_s), load(pivots_h, pivots_v), load(nbr_h, nbr_s),
                load(par_h, par_s)]
    in_i = [load(interp_h.at[b], interp_v.at[b]) for b in range(BOXES_HERE)]
    in_r = [load(redinv_h.at[b], redinv_v.at[b]) for b in range(BOXES_HERE)]
    barrier = pltpu.get_barrier_semaphore()
    partners = ([(row(dx, 0), gy) for dx in range(1, XS)]
                + [(row(0, dz), gy) for dz in range(1, ZS)] + lanes)
    for device in partners:
        pl.semaphore_signal(barrier, inc=1, device_id=device, device_id_type=MESH)

    in_low, in_n = [], []

    def load_box(b):
        in_low.append(load(back_h.at[b, :, pl.ds(0, RB)], back_v.at[b, :, pl.ds(0, RB)]))
        in_n.append(load(near_h.at[b], near_v.at[b]))


    load_box(0)
    in_small[0].wait()
    in_small[1].wait()
    upd_a[ENTRIES] = jnp.zeros((RA, K), F32)
    upd_b[ENTRIES] = jnp.zeros((RB, K), F32)

    for copy in in_i + in_r:
        copy.wait()
    load_box(1)
    make_eliminators(ranks_s, pivots_v, interp_v, redinv_v, elim_v)
    in_high = [load(back_h.at[b, :, pl.ds(RB, RA)], back_v.at[b, :, pl.ds(RB, RA)])
               for b in range(BOXES_HERE)]
    in_s = load(self_h, self_v)

    in_small[2].wait()
    in_small[3].wait()
    slots = lax.broadcasted_iota(jnp.int32, (1, K), 1)
    for b in range(BOXES_HERE):
        table = jnp.full((1, K), ENTRIES, jnp.int32)
        for n in range(NBR):
            target = nbr_s[b, n]
            slot = (target // (BOXES_HERE * YS * 2)) * BOXES_HERE + target % BOXES_HERE
            table = jnp.where(slots == slot, b * NBR + n, table)
        tab_v[b:b + 1, :] = table
    for b in range(BOXES_HERE):
        own_par[b:b + 1, :] = jnp.full((1, K), par_s[b], jnp.int32)
    tab_copy = pltpu.make_async_copy(tab_v, tab_s, tab_sem.at[0])
    tab_copy.start()
    own_copy = pltpu.make_async_copy(own_par, all_par.at[gy], tab_sem.at[1])
    own_copy.start()
    def products(upd, first, rows, needs):
        for b in range(BOXES_HERE):
            for copies in needs:
                copies[b].wait()

            wide = back_v[b, :, first:first + rows].reshape(NBR * rows, PTS)
            lifted = jnp.dot(wide, elim_v[b], preferred_element_type=F32).astype(BF)
            for n in range(NBR):
                upd[b * NBR + n] = jnp.dot(lifted[n * rows:(n + 1) * rows], near_v[b, n],
                                           preferred_element_type=F32)

    def order(p):
        return ZS // 2 + p // 2 if p % 2 == 0 else ZS // 2 - 1 - p // 2

    def gathered(upd, kx, kz):
        there = ((x + kx) % XS) * ZS + (z + kz) % ZS
        s = BOXES_HERE * there
        return [(upd[tab_s[0, s + q]] + upd[tab_s[1, s + q]]).astype(BF)
                for q in range(BOXES_HERE)]

    def assemble_b(*kzs):
        def one(kx, carry):
            for kz in kzs:
                for q, value in enumerate(gathered(upd_b, kx, kz)):
                    out_b[kz, kx, q] = value
            return carry

        lax.fori_loop(0, XS, one, 0)

    def assemble_a(g):
        def one(kx, carry):
            for p in range(g * GROUP, (g + 1) * GROUP):
                for q, value in enumerate(gathered(upd_a, kx, order(p))):
                    out_a[kx, p, q] = value
            return carry

        lax.fori_loop(0, XS, one, 0)

    mail = Mail(send_sem, recv_sem)

    hop = {}
    long_way = [(0, 0), (1, 2), (0, 1), (1, 3)]
    short_way = [(0, 2), (1, 0), (0, 3), (1, 1)]
    ways = [pair for both in zip(long_way, short_way) for pair in both]

    def toward(d, k):
        return k if d == 0 else ZS - k

    def post_b(d, h, k, links):
        hop[d, h, k] = mail.post(out_b.at[toward(d, k), h], rzb.at[d, h, k - 1],
                                 (row(0, toward(d, links)), gy))

    def pass_b(d, h, k):
        total = out_b[toward(d, k), h].astype(F32)
        if k == 2 and (d, h) in long_way:
            hop[d, h, 4].wait_recv()
            total = total + rzb[d, h, 3].astype(F32)
        hop[d, h, k + 1].wait_recv()
        out_b[toward(d, k), h] = (total + rzb[d, h, k].astype(F32)).astype(BF)
        post_b(d, h, k, 1)

    cross = {}

    def post_a(g):
        span = pl.ds(g * GROUP, GROUP)
        for kx in (2, 1, 3):
            cross[g, kx] = mail.post(out_a.at[kx, span], rxa.at[kx - 1, span], (row(kx, 0), gy))

    products(upd_b, 0, RB, (in_low, in_n))
    tab_copy.wait()
    assemble_b(4)
    pl.semaphore_wait(barrier, len(partners))
    for d, h in long_way:
        post_b(d, h, 4, 2)
    assemble_b(3, 5)
    for d, h in ways:
        post_b(d, h, 3, 1)
    assemble_b(2, 6)
    assemble_b(1, 7, 0)

    products(upd_a, RB, RA, (in_high,))
    for g in range(ZS // GROUP):
        assemble_a(g)
        post_a(g)
    par_mail = [mail.post(own_par, all_par.at[gy], device) for device in lanes]

    down = {}

    def settle_a(g):
        for kx in (1, 3, 2):
            cross[g, kx].wait_recv()
        for p in range(g * GROUP, (g + 1) * GROUP):
            total = (out_a[0, p].astype(F32) + rxa[0, p].astype(F32)
                     + rxa[1, p].astype(F32) + rxa[2, p].astype(F32))
            kz = order(p)
            if kz:
                sza[p] = total.astype(BF)
                down[p] = mail.post(sza.at[p], rza.at[p], (row(0, kz), gy))
            else:
                acc_a[...] = total

    for d, h in ways:
        pass_b(d, h, 2)
    for d, h in ways:
        pass_b(d, h, 1)
    settle_a(0)
    side = {}
    for h in (2, 1, 3, 0):
        for d in range(2):
            hop[d, h, 1].wait_recv()
        total = out_b[0, h].astype(F32) + rzb[0, h, 0].astype(F32) + rzb[1, h, 0].astype(F32)
        if h:
            sxb[h - 1] = total.astype(BF)
            side[h] = mail.post(sxb.at[h - 1], rxb.at[h - 1], (row(h, 0), gy))
        else:
            acc_b[...] = total
    settle_a(1)
    settle_a(2)
    settle_a(3)

    in_s.wait()
    def finish(gath, first, rows, total):
        j = lax.broadcasted_iota(jnp.int32, (rows, K), 0) + first
        l = lax.broadcasted_iota(jnp.int32, (rows, K), 1)
        for q in range(BOXES_HERE):
            rank = ranks_s[q]
            merged = jnp.where((j < rank) & (l < rank), self_v[q, first:first + rows] + total[q], 0.0)
            gath[gy, q] = merged.astype(BF)
        return [mail.post(gath.at[gy], gath.at[gy], device)
                for device in [(gx, lane(dy, dc)) for dy, dc in
                               ((2, 1), (2, 0), (1, 1), (3, 1), (1, 0), (3, 0), (0, 1))]]

    total = acc_b[...]
    for h in (1, 3, 2):
        side[h].wait_recv()
        total = total + rxb[h - 1].astype(F32)
    sent_b = finish(gath_b, 0, RB, total)

    total = acc_a[...]
    for p in range(ZS - 1):
        down[p].wait_recv()
        total = total + rza[p].astype(F32)
    sent_a = finish(gath_a, RB, RA, total)

    own_copy.wait()
    for copy in par_mail:
        copy.wait_recv()
    par_copy = pltpu.make_async_copy(all_par, par_tab, tab_sem.at[2])
    par_copy.start()

    par_copy.wait()

    first_row = gx * (YS * 2 * BOXES_HERE) + gy * BOXES_HERE
    found = []
    for q in range(BOXES_HERE):
        found_lane, found_slot = jnp.int32(0), jnp.int32(0)
        for k in range(YS * 2):
            for s in range(BOXES_HERE):
                hit = par_tab[k, s, 0] == first_row + q
                found_lane = jnp.where(hit, k, found_lane)
                found_slot = jnp.where(hit, s, found_slot)
        found.append((found_lane, found_slot))
    for copy in mail.made:
        copy.wait_send()
    for copy in sent_b + sent_a:
        copy.wait_recv()
    for q in range(BOXES_HERE):
        out_ref[q, 0:RB] = gath_b[found[q][0], found[q][1]]
        out_ref[q, RB:K] = gath_a[found[q][0], found[q][1]]


def body(self_blk, near, back, interp, redinv, ranks, pivots, neighbors, parent):
    hbm = pl.BlockSpec(memory_space=pl.ANY)
    a_blk, b_blk = (BOXES_HERE, RA, K), (BOXES_HERE, RB, K)
    rows = pl.pallas_call(
        kernel,
        out_shape=jax.ShapeDtypeStruct((BOXES_HERE, K, K), BF),
        in_specs=[hbm] * 9,
        out_specs=pl.BlockSpec(memory_space=pltpu.VMEM),
        scratch_shapes=[
            pltpu.VMEM((BOXES_HERE, K, K), F32),
            pltpu.VMEM((BOXES_HERE, NBR, PTS, K), BF),
            pltpu.VMEM((BOXES_HERE, NBR, K, PTS), BF),
            pltpu.VMEM((BOXES_HERE, K, PTS), BF),
            pltpu.VMEM((BOXES_HERE, PTS, PTS), BF),
            pltpu.VMEM((BOXES_HERE, PTS, PTS), BF),
            pltpu.VMEM((ENTRIES + 1, RA, K), F32),
            pltpu.VMEM((ENTRIES + 1, RB, K), F32),
            pltpu.VMEM((BOXES_HERE, K), jnp.int32),
            pltpu.SMEM((BOXES_HERE, K), jnp.int32),
            pltpu.VMEM((BOXES_HERE, K), jnp.int32),
            pltpu.VMEM((YS * 2, BOXES_HERE, K), jnp.int32),
            pltpu.SMEM((YS * 2, BOXES_HERE, K), jnp.int32),
            pltpu.SMEM((BOXES_HERE,), jnp.int32),
            pltpu.VMEM((BOXES_HERE, K), jnp.int32),
            pltpu.SMEM((BOXES_HERE, NBR), jnp.int32),
            pltpu.SMEM((BOXES_HERE,), jnp.int32),
            pltpu.VMEM((XS, ZS) + a_blk, BF),
            pltpu.VMEM((ZS, XS) + b_blk, BF),
            pltpu.VMEM((XS - 1, ZS) + a_blk, BF),
            pltpu.VMEM((ZS - 1,) + a_blk, BF),
            pltpu.VMEM((ZS - 1,) + a_blk, BF),
            pltpu.VMEM(a_blk, F32),
            pltpu.VMEM((2, XS, ZS // 2) + b_blk, BF),
            pltpu.VMEM((XS - 1,) + b_blk, BF),
            pltpu.VMEM((XS - 1,) + b_blk, BF),
            pltpu.VMEM(b_blk, F32),
            pltpu.VMEM((YS * 2,) + a_blk, BF),
            pltpu.VMEM((YS * 2,) + b_blk, BF),
            pltpu.SemaphoreType.DMA((15,)),
            pltpu.SemaphoreType.DMA((3,)),
            pltpu.SemaphoreType.DMA((MESSAGES,)),
            pltpu.SemaphoreType.DMA((MESSAGES,)),
        ],
        compiler_params=pltpu.CompilerParams(
            collective_id=0, has_side_effects=True, vmem_limit_bytes=VMEM_LIMIT),
    )(self_blk, near, back, interp, redinv, ranks, pivots, neighbors, parent)
    return rows.astype(F32)


def solution(mesh):
    wide = ("gx", "gy")
    placed = (
        P(wide, None, None),
        P(wide, None, None, None),
        P(wide, None, None, None),
        P(wide, None, None),
        P(wide, None, None),
        P(wide),
        P(wide, None),
        P(wide, None),
        P(wide),
    )
    return jax.shard_map(
        body, mesh=mesh, in_specs=placed, out_specs=P(wide, None, None), check_vma=False
    )
```
